32 devices in a mesh: member: 4 (over y, x), dp: 8 (over z, core).
Axes of the slice: x: 2, y: 2, z: 4, core: 2. Of those that a mesh axis runs over, the one named last changes fastest.
Arguments:
- inputs: bfloat16 [4, 6144, 1024], P('member', 'dp'), may hold values from -6 to 6
- w_in: bfloat16 [4, 1024, 4096], P('member', 'dp'), may hold values from -6 to 6
- w_out: bfloat16 [4, 4096, 1024], P('member', 'dp'), may hold values from -6 to 6
- cotangent: bfloat16 [4, 6144, 1024], P('member', 'dp'), may hold values from -6 to 6
Outputs:
- merged_in: bfloat16 [1024, 4096], P('dp', 'member')
- merged_out: bfloat16 [4096, 1024], P('dp', 'member')
The draws below stay inside these ranges and needn't reach their ends.
All inputs are finite; a program needn't handle non-finite values.
Results may differ from the reference program's by a relative error of at most 0.018.
Values may be sent and summed in bfloat16 or wider, within the bound.
No kernel may reach another device: no remote copies, remote signals or barrier semaphores. Data moves between devices by JAX's collectives and lax.ppermute only.
A program may use at most 128 MiB of HBM per device.

```python
import jax
import jax.numpy as jnp
from jax import lax

D = 1024
FF = 4096
TOK_DEV = 768
MEMBERS = 4
TOKENS = 6144
N_DP = 8


def with_spikes(drawn, rng, source, target, shards_of, factor):
    def block_of(dim):
        return (jnp.arange(drawn.shape[dim]) // (drawn.shape[dim] // shards_of)).reshape((-1,) + (1,) * (drawn.ndim - 1 - dim))

    one_side = jax.random.permutation(rng, shards_of)[block_of(target)]
    other_side = (block_of(target) + shards_of // 2) % shards_of
    return jnp.where((block_of(source) == one_side) | (block_of(source) == other_side), factor * drawn, drawn)


def levels(own_key, dims, cuts, low, high):
    gain = 1.0
    for dim, parts in cuts:
        heights = jax.random.uniform(jax.random.fold_in(jax.random.fold_in(own_key, 6), dim), (parts,), jnp.float32, low / len(cuts), high / len(cuts))
        gain = gain * jnp.repeat(jnp.exp(heights), dims[dim] // parts).reshape((-1,) + (1,) * (len(dims) - 1 - dim))
    return gain


def gaussian(key, extent, deviation, limit, shards=(), kind=jnp.bfloat16):
    values = deviation * jax.random.normal(key, extent, jnp.float32)
    if shards:
        values = values * levels(key, extent, shards, -0.22, 0.18)
    return jnp.clip(values, -limit, limit).astype(kind)


def noise_with(rng, extent, width, reach, cuts, heavy, held_as=jnp.bfloat16):
    array = width * jax.random.normal(rng, extent, jnp.float32)
    if cuts:
        array = array * levels(rng, extent, cuts, -0.22, 0.18)
    return jnp.clip(with_spikes(array, jax.random.fold_in(rng, 3), *heavy), -reach, reach).astype(held_as)


def setup_inputs(seed: int = 0) -> dict:
    seeds = jax.random.split(jax.random.key(seed), 5)
    inputs = noise_with(seeds[0], (MEMBERS, TOKENS, D), 1.0, 6.0, ((0, 4), (1, 8)), (1, 2, 8, 2.0))
    w_in = gaussian(seeds[1], (MEMBERS, D, FF), 1.0, 6.0, ((0, 4), (1, 8)))
    w_out = gaussian(seeds[2], (MEMBERS, FF, D), 1.0, 6.0, ((0, 4), (1, 8)))
    cotangent = noise_with(seeds[3], (MEMBERS, TOKENS, D), 1.0, 6.0, ((0, 4), (1, 8)), (1, 2, 8, 2.0))
    return {"inputs": inputs, "w_in": w_in, "w_out": w_out, "cotangent": cotangent}


def member_fisher(x_all, g_all, w1, w2):
    scale_in = float(D) ** -0.5
    scale_out = float(FF) ** -0.5
    x_blocks = x_all.reshape(N_DP, TOK_DEV, D)
    g_blocks = g_all.reshape(N_DP, TOK_DEV, D)

    def block_step(carry, pieces):
        f_in, f_out = carry
        xb, gb = pieces
        pre = jnp.dot(xb, w1, preferred_element_type=jnp.float32) * scale_in
        sig = jax.nn.sigmoid(pre)
        hidden = (pre * sig).astype(jnp.bfloat16)
        back = jnp.dot(gb, w2.T, preferred_element_type=jnp.float32)
        grad_hidden = (back * scale_out * (sig * (1.0 + pre * (1.0 - sig)))).astype(jnp.bfloat16)
        sq_in = jnp.square(xb.astype(jnp.float32)).astype(jnp.bfloat16)
        sq_grad = jnp.square(grad_hidden.astype(jnp.float32)).astype(jnp.bfloat16)
        sq_hidden = jnp.square(hidden.astype(jnp.float32)).astype(jnp.bfloat16)
        sq_cot = jnp.square(gb.astype(jnp.float32)).astype(jnp.bfloat16)
        part_in = jnp.dot(sq_in.T, sq_grad, preferred_element_type=jnp.float32)
        part_out = jnp.dot(sq_hidden.T, sq_cot, preferred_element_type=jnp.float32)
        part_in = lax.optimization_barrier(part_in.astype(jnp.bfloat16)).astype(jnp.float32)
        part_out = lax.optimization_barrier(part_out.astype(jnp.bfloat16)).astype(jnp.float32)
        return (f_in + part_in, f_out + part_out), None

    init = (jnp.zeros((D, FF), jnp.float32), jnp.zeros((FF, D), jnp.float32))
    (f_in, f_out), _ = lax.scan(block_step, init, (x_blocks, g_blocks))
    return f_in, f_out


def rounded(value):
    return lax.optimization_barrier(value.astype(jnp.bfloat16)).astype(jnp.float32)


def reference(inputs, w_in, w_out, cotangent):
    num_in = jnp.zeros((D, FF), jnp.float32)
    den_in = jnp.zeros((D, FF), jnp.float32)
    num_out = jnp.zeros((FF, D), jnp.float32)
    den_out = jnp.zeros((FF, D), jnp.float32)
    for member in range(MEMBERS):
        f_in, f_out = member_fisher(inputs[member], cotangent[member], w_in[member], w_out[member])
        num_in = num_in + rounded(f_in * w_in[member].astype(jnp.float32))
        den_in = den_in + rounded(f_in)
        num_out = num_out + rounded(f_out * w_out[member].astype(jnp.float32))
        den_out = den_out + rounded(f_out)
    merged_in = (num_in / (den_in + 1e-6)).astype(jnp.bfloat16)
    merged_out = (num_out / (den_out + 1e-6)).astype(jnp.bfloat16)
    return (merged_in, merged_out)
```

```python
import functools

import jax
import jax.numpy as jnp
from jax import lax
from jax.experimental import pallas as pl
from jax.experimental.pallas import tpu as pltpu
from jax.sharding import PartitionSpec as P

CHUNKS = 4
F32 = jnp.float32
BF16 = jnp.bfloat16


def swap(value, axis, flip):
    size = lax.axis_size(axis)
    return lax.ppermute(value, axis, [(i, i ^ flip) for i in range(size)])


def pick(value, index, axis):
    return lax.dynamic_index_in_dim(value, index, axis, keepdims=False)


def nt(left, right):
    return lax.dot_general(left, right, (((1,), (1,)), ((), ())), preferred_element_type=F32)


def tn(left, right):
    return lax.dot_general(left, right, (((0,), (0,)), ((), ())), preferred_element_type=F32)


def chunk_kernel(cfg, where_ref, *refs):
    members, chips, rows, blocks, scale_in, scale_out = cfg
    refs = list(refs)
    take = lambda count: [refs.pop(0) for _ in range(count)]
    tok_refs = [take(len(sizes)) for sizes in blocks]
    cot_refs = [take(len(sizes)) for sizes in blocks]
    groups = chips // 2
    win_refs = take(groups)
    wout_refs = take(groups)
    in_send, in_keep, out_send, out_keep = take(4)
    tok, cot, win, wout, acc_in, acc_out, tok_sem, cot_sem = take(8)
    width = win.shape[1]
    part = width // chips
    cols = width // members
    me, chip = where_ref[0], where_ref[1]

    def copies(b):
        out = []
        start = 0
        for p, size in enumerate(blocks[b]):
            to = pl.ds(start, size)
            out.append(pltpu.make_async_copy(tok_refs[b][p], tok.at[b, to], tok_sem.at[b, p]))
            out.append(pltpu.make_async_copy(cot_refs[b][p], cot.at[b, to], cot_sem.at[b, p]))
            start += size
        return out

    for b in range(len(blocks)):
        for copy in copies(b):
            copy.start()

    for g in range(groups):
        for h in range(2):
            other = chip ^ (2 * g + h)
            wout[pl.ds(pl.multiple_of(other * rows, rows), rows), :] = wout_refs[g][h]
            lane = pl.ds(pl.multiple_of(other * part, part), part)
            for m in range(members):
                win[m * rows : (m + 1) * rows, lane] = win_refs[g][h, m]

    for b in range(len(blocks)):
        for copy in copies(b):
            copy.wait()
        x = tok[b]
        g = cot[b]
        pre = nt(x, win[...]) * scale_in
        back = nt(g, wout[...]) * scale_out
        sig = jax.nn.sigmoid(pre)
        hidden = (pre * sig).astype(BF16)
        grad = (back * (sig * (1.0 + pre * (1.0 - sig)))).astype(BF16)
        part_in = tn(grad * grad, x * x)
        part_out = tn(hidden * hidden, g * g)
        if b == 0:
            acc_in[...] = part_in
            acc_out[...] = part_out
        else:
            acc_in[...] += part_in
            acc_out[...] += part_out

    bits = members.bit_length() - 1
    for m in range(members):
        rel = me ^ m
        low = rel & 1
        rest = rel >> 1
        span = slice(m * rows, (m + 1) * rows)
        den = acc_in[span, :]
        num = (den * win[span, :].astype(F32)).astype(BF16)
        den = den.astype(BF16)

        @pl.when(low == 1)
        def _():
            in_send[rest, 0] = num
            in_send[rest, 1] = den

        @pl.when(low == 0)
        def _():
            in_keep[rest, 0] = num
            in_keep[rest, 1] = den

        high = rel >> (bits - 1)
        rest2 = rel & (members // 2 - 1)
        lane = slice(m * cols, (m + 1) * cols)
        den2 = acc_out[:, lane]
        num2 = (den2 * wout[:, lane].astype(F32)).astype(BF16)
        den2 = den2.astype(BF16)

        @pl.when(high == 1)
        def _():
            out_send[rest2, 0] = num2
            out_send[rest2, 1] = den2

        @pl.when(high == 0)
        def _():
            out_keep[rest2, 0] = num2
            out_keep[rest2, 1] = den2


def chunk_call(where, tok_parts, cot_parts, win_parts, wout_parts, members, chips, scales):
    rows, width = wout_parts[0].shape[1:]
    blocks = tuple(tuple(p.shape[0] for p in parts) for parts in tok_parts)
    most = max(len(b) for b in blocks)
    height = sum(blocks[0])
    n_rows = members * rows
    half = members // 2
    any_spec = pl.BlockSpec(memory_space=pl.ANY)
    vmem = pl.BlockSpec(memory_space=pltpu.VMEM)
    flat_tok = [p for parts in tok_parts for p in parts]
    flat_cot = [p for parts in cot_parts for p in parts]
    shape_in = jax.ShapeDtypeStruct((half, 2, rows, width), BF16)
    shape_out = jax.ShapeDtypeStruct((half, 2, n_rows, width // members), BF16)
    cfg = (members, chips, rows, blocks) + scales
    tokens = sum(sum(b) for b in blocks)
    return pl.pallas_call(
        functools.partial(chunk_kernel, cfg),
        out_shape=[shape_in, shape_in, shape_out, shape_out],
        in_specs=[pl.BlockSpec(memory_space=pltpu.SMEM)]
        + [any_spec] * (len(flat_tok) + len(flat_cot))
        + [vmem] * (len(win_parts) + len(wout_parts)),
        out_specs=[vmem] * 4,
        scratch_shapes=[
            pltpu.VMEM((len(blocks), height, width), BF16),
            pltpu.VMEM((len(blocks), height, width), BF16),
            pltpu.VMEM((n_rows, width), BF16),
            pltpu.VMEM((n_rows, width), BF16),
            pltpu.VMEM((n_rows, width), F32),
            pltpu.VMEM((n_rows, width), F32),
            pltpu.SemaphoreType.DMA((len(blocks), most)),
            pltpu.SemaphoreType.DMA((len(blocks), most)),
        ],
        compiler_params=pltpu.CompilerParams(vmem_limit_bytes=56 * 1024 * 1024),
        cost_estimate=pl.CostEstimate(
            flops=8 * tokens * n_rows * width,
            transcendentals=2 * tokens * n_rows,
            bytes_accessed=4 * tokens * width + 12 * n_rows * width,
        ),
    )(where, *flat_tok, *flat_cot, *win_parts, *wout_parts)


def add(left, right):
    return (left.astype(F32) + right.astype(F32)).astype(BF16)


def over_members(send, keep, flips):
    for step, flip in enumerate(flips):
        got = swap(send, "member", flip)
        if step + 1 < len(flips):
            half = keep.shape[0] // 2
            send = add(keep[half:], got[half:])
            keep = add(keep[:half], got[:half])
    return keep[0].astype(F32) + got[0].astype(F32)


def on_device(inputs, w_in, w_out, cotangent):
    members, n_dp = lax.axis_size("member"), lax.axis_size("dp")
    me, dp = lax.axis_index("member"), lax.axis_index("dp")
    core, low, group, chip = dp & 1, (dp >> 1) & 1, dp >> 2, dp >> 1
    chips, groups = n_dp // 2, n_dp // 4
    tok, cot = inputs[0], cotangent[0]
    n_tok, width = tok.shape
    d_own = width // n_dp
    ff = w_in.shape[2]
    per_s = ff // members // 4
    k_n = CHUNKS
    rows = per_s // k_n
    scales = (float(width) ** -0.5, float(ff) ** -0.5)
    bits = members.bit_length() - 1
    up = [1 << b for b in range(bits)]
    down = up[::-1]

    half = n_tok // 2
    tok_z = [swap(tok[:half], "dp", 2), swap(tok[half:], "dp", 2)]
    cot_z = [swap(cot[:half], "dp", 2), swap(cot[half:], "dp", 2)]
    tok_parts = [[tok], [swap(tok, "dp", 1)], tok_z, [swap(p, "dp", 1) for p in tok_z]]
    cot_parts = [[cot], [swap(cot, "dp", 1)], cot_z, [swap(p, "dp", 1) for p in cot_z]]

    wt = w_in[0].T.reshape(members, 2, 2, k_n, rows, d_own)
    mine, theirs = pick(wt, core, 2), pick(wt, 1 - core, 2)
    got = swap(theirs, "dp", 1)
    both = jnp.where(
        core == 0, jnp.concatenate([mine, got], -1), jnp.concatenate([got, mine], -1)
    )
    both = both.transpose(1, 2, 0, 3, 4)
    win_keep = pick(both, low, 0)
    win_got = swap(pick(both, 1 - low, 0), "dp", 2)

    wo = w_out[0].reshape(2, k_n, rows, width)
    mine, theirs = pick(wo, core, 0), pick(wo, 1 - core, 0)
    got = swap(theirs, "dp", 1)
    wout_keep = jnp.where(low == core, mine, got)
    wout_got = swap(jnp.where(low == core, got, mine), "dp", 2)

    where = jnp.stack([me, chip]).astype(jnp.int32)
    merged_in, merged_out = [], []
    for k in range(k_n):
        win_parts = [jnp.stack([win_keep[k], win_got[k]])]
        wout_parts = [jnp.stack([wout_keep[k], wout_got[k]])]
        flip = 4
        while flip < n_dp:
            win_parts = win_parts + [swap(p, "dp", flip) for p in win_parts]
            wout_parts = wout_parts + [swap(p, "dp", flip) for p in wout_parts]
            flip *= 2
        in_send, in_keep, out_send, out_keep = chunk_call(
            where, tok_parts, cot_parts, win_parts, wout_parts, members, chips, scales
        )
        y_in = over_members(in_send, in_keep, up)
        y_out = over_members(out_send, out_keep, down)
        y_in = y_in.reshape(2, rows, groups, 4 * d_own)
        y_out = y_out.reshape(2, groups, 2 * rows, width // members)
        left = groups
        while left > 1:
            left //= 2
            top = (group // left) & 1
            take = lambda v, side, axis: lax.dynamic_slice_in_dim(v, side * left, left, axis)
            got_in = swap(take(y_in, 1 - top, 2).astype(BF16), "dp", 4 * left)
            got_out = swap(take(y_out, 1 - top, 1).astype(BF16), "dp", 4 * left)
            y_in = take(y_in, top, 2) + got_in.astype(F32)
            y_out = take(y_out, top, 1) + got_out.astype(F32)
        y_in = y_in.reshape(2, rows, 4 * d_own)
        y_out = y_out.reshape(2, 2, rows, width // members)
        merged_in.append((y_in[0] / (y_in[1] + 1e-6)).astype(BF16))
        merged_out.append((y_out[0] / (y_out[1] + 1e-6)).astype(BF16))

    m_in = jnp.concatenate(merged_in, 0).reshape(per_s, 2, 2 * d_own)
    got = swap(pick(m_in, 1 - low, 1), "dp", 2)
    m_in = jnp.stack([pick(m_in, low, 1), got]).reshape(2, per_s, 2, d_own)
    got = swap(pick(m_in, 1 - core, 2), "dp", 1)
    m_in = jnp.stack([pick(m_in, core, 2), got], 1)
    m_in = jnp.where(low == 0, m_in, m_in[::-1])
    m_in = jnp.where(core == 0, m_in, m_in[:, ::-1])
    out_in = m_in.reshape(4 * per_s, d_own).T

    m_out = jnp.concatenate(merged_out, 1)
    got = swap(pick(m_out, 1 - low, 0), "dp", 2)
    mine = pick(m_out, low, 0)
    same = low == core
    stay = jnp.where(same, mine, got)
    got = swap(jnp.where(same, got, mine), "dp", 1)
    out_out = jnp.where(
        core == 0, jnp.concatenate([stay, got]), jnp.concatenate([got, stay])
    )
    return out_in, out_out


def solution(mesh):
    spec = P("member", "dp", None)
    return jax.shard_map(
        on_device,
        mesh=mesh,
        in_specs=(spec, spec, spec, spec),
        out_specs=(P("dp", "member"), P("dp", "member")),
        check_vma=False,
    )
```

```python
import functools

import jax
import jax.numpy as jnp
from jax import lax
from jax.experimental import pallas as pl
from jax.experimental.pallas import tpu as pltpu
from jax.sharding import PartitionSpec as P

CHUNKS = 4
F32 = jnp.float32
BF16 = jnp.bfloat16


def swap(value, axis, flip):
    size = lax.axis_size(axis)
    return lax.ppermute(value, axis, [(i, i ^ flip) for i in range(size)])


def after(value, *others):
    return lax.optimization_barrier((value,) + others)[0]


def pick(value, index, axis):
    return lax.dynamic_index_in_dim(value, index, axis, keepdims=False)


def nt(left, right):
    return lax.dot_general(left, right, (((1,), (1,)), ((), ())), preferred_element_type=F32)


def tn(left, right):
    return lax.dot_general(left, right, (((0,), (0,)), ((), ())), preferred_element_type=F32)


def chunk_kernel(cfg, where_ref, *refs):
    members, chips, rows, blocks, scale_in, scale_out = cfg
    refs = list(refs)
    take = lambda count: [refs.pop(0) for _ in range(count)]
    tok_refs = [take(len(sizes)) for sizes in blocks]
    cot_refs = [take(len(sizes)) for sizes in blocks]
    w_refs = take(chips // 2)
    outs = [take(2), take(2)]
    tok, cot, w_all, acc, stage, tok_sem, cot_sem, w_sem, out_sem = take(9)
    width = w_all.shape[2]
    part = width // chips
    cols = width // members
    me, chip = where_ref[0], where_ref[1]

    def fetch(b):
        start = 0
        for p, size in enumerate(blocks[b]):
            to = pl.ds(start, size)
            pltpu.make_async_copy(tok_refs[b][p], tok.at[b, to], tok_sem.at[b]).start()
            pltpu.make_async_copy(cot_refs[b][p], cot.at[b, to], cot_sem.at[b]).start()
            start += size

    for g, w_ref in enumerate(w_refs):
        for h in range(2):
            other = chip ^ (2 * g + h)
            down = pl.ds(pl.multiple_of(other * rows, rows), rows)
            lane = pl.ds(pl.multiple_of(other * part, part), part)
            pltpu.make_async_copy(w_ref.at[h, 1], w_all.at[1, down], w_sem).start()
            for m in range(members):
                pltpu.make_async_copy(
                    w_ref.at[h, 0, :, pl.ds(m * part, part)],
                    w_all.at[0, pl.ds(m * rows, rows), lane],
                    w_sem,
                ).start()
    fetch(0)
    fetch(1)
    pltpu.make_async_copy(w_all, w_all, w_sem).wait()

    def body(b, carry):
        for n in range(2, len(blocks)):

            @pl.when(b == n - 2)
            def _():
                fetch(n)

        pltpu.make_async_copy(tok.at[b], tok.at[b], tok_sem.at[b]).wait()
        pltpu.make_async_copy(cot.at[b], cot.at[b], cot_sem.at[b]).wait()
        x = tok[b]
        g = cot[b]
        pre = nt(x, w_all[0]) * scale_in
        back = nt(g, w_all[1]) * scale_out
        sig = jax.nn.sigmoid(pre)
        hidden = (pre * sig).astype(BF16)
        grad = (back * (sig * (1.0 + pre * (1.0 - sig)))).astype(BF16)
        part_in = tn(grad * grad, x * x)
        part_out = tn(hidden * hidden, g * g)

        @pl.when(b == 0)
        def _():
            acc[0] = part_in
            acc[1] = part_out

        @pl.when(b > 0)
        def _():
            acc[0] += part_in
            acc[1] += part_out

        return carry

    lax.fori_loop(0, len(blocks), body, 0)

    top = members // 2
    for m in range(members):
        rel = me ^ m
        places = [(rel & 1, rel >> 1), ((rel >= top).astype(jnp.int32), rel & (top - 1))]
        span = slice(m * rows, (m + 1) * rows)
        lane = slice(m * cols, (m + 1) * cols)
        den = acc[0, span, :]
        stage[0, m, :rows] = (den * w_all[0, span, :].astype(F32)).astype(BF16)
        stage[0, m, rows:] = den.astype(BF16)
        den = acc[1, :, lane]
        num = (den * w_all[1, :, lane].astype(F32)).astype(BF16)
        den = den.astype(BF16)
        for q in range(members):
            to = slice(q * cols, (q + 1) * cols)
            own = slice(q * rows, (q + 1) * rows)
            stage[1, m, :rows, to] = num[own]
            stage[1, m, rows:, to] = den[own]
        for io in range(2):
            for value in range(2):
                side, rest = places[io]

                @pl.when(side == value)
                def _():
                    pltpu.make_async_copy(
                        stage.at[io, m], outs[io][value].at[rest], out_sem
                    ).start()

    pltpu.make_async_copy(stage, stage, out_sem).wait()


def chunk_call(where, tok_parts, cot_parts, w_parts, members, chips, scales):
    rows, width = w_parts[0].shape[2:]
    blocks = tuple(tuple(p.shape[0] for p in parts) for parts in tok_parts)
    height = sum(blocks[0])
    n_rows = members * rows
    any_spec = pl.BlockSpec(memory_space=pl.ANY)
    flat_tok = [p for parts in tok_parts for p in parts]
    flat_cot = [p for parts in cot_parts for p in parts]
    shape = jax.ShapeDtypeStruct((members // 2, 2 * rows, width), BF16)
    cfg = (members, chips, rows, blocks) + scales
    tokens = sum(sum(b) for b in blocks)
    return pl.pallas_call(
        functools.partial(chunk_kernel, cfg),
        out_shape=[shape] * 4,
        in_specs=[pl.BlockSpec(memory_space=pltpu.SMEM)]
        + [any_spec] * (len(flat_tok) + len(flat_cot) + len(w_parts)),
        out_specs=[any_spec] * 4,
        scratch_shapes=[
            pltpu.VMEM((len(blocks), height, width), BF16),
            pltpu.VMEM((len(blocks), height, width), BF16),
            pltpu.VMEM((2, n_rows, width), BF16),
            pltpu.VMEM((2, n_rows, width), F32),
            pltpu.VMEM((2, members, 2 * rows, width), BF16),
            pltpu.SemaphoreType.DMA((len(blocks),)),
            pltpu.SemaphoreType.DMA((len(blocks),)),
            pltpu.SemaphoreType.DMA,
            pltpu.SemaphoreType.DMA,
        ],
        compiler_params=pltpu.CompilerParams(vmem_limit_bytes=56 * 1024 * 1024),
        cost_estimate=pl.CostEstimate(
            flops=8 * tokens * n_rows * width,
            transcendentals=2 * tokens * n_rows,
            bytes_accessed=4 * tokens * width + 12 * n_rows * width,
        ),
    )(where, *flat_tok, *flat_cot, *w_parts)


def add(left, right):
    return (left.astype(F32) + right.astype(F32)).astype(BF16)


def over_members(send, keep, flips):
    for step, flip in enumerate(flips):
        got = swap(send, "member", flip)
        if step + 1 < len(flips):
            half = keep.shape[0] // 2
            send = add(keep[half:], got[half:])
            keep = add(keep[:half], got[:half])
            second = send if step == 0 else second
    return keep[0].astype(F32) + got[0].astype(F32), second


def half_of(value, side):
    size = value.shape[-1] // 2
    return lax.dynamic_slice_in_dim(value, side * size, size, value.ndim - 1)


def on_device(inputs, w_in, w_out, cotangent):
    members, n_dp = lax.axis_size("member"), lax.axis_size("dp")
    me, dp = lax.axis_index("member"), lax.axis_index("dp")
    core, low, chip = dp & 1, (dp >> 1) & 1, dp >> 1
    chips = n_dp // 2
    tok, cot = inputs[0], cotangent[0]
    n_tok, width = tok.shape
    d_own = width // n_dp
    ff = w_in.shape[2]
    per_s = ff // members // 4
    k_n = CHUNKS
    rows = per_s // k_n
    scales = (float(width) ** -0.5, float(ff) ** -0.5)

    wt = w_in[0].T.reshape(members, 2, 2, k_n, rows, d_own).transpose(2, 1, 3, 4, 0, 5)
    mine, theirs = pick(wt, core, 0), pick(wt, 1 - core, 0)
    got = swap(theirs, "dp", 1)
    both = jnp.where(
        core == 0, jnp.concatenate([mine, got], -1), jnp.concatenate([got, mine], -1)
    ).reshape(2, k_n, rows, members * 2 * d_own)
    wo = w_out[0].reshape(2, k_n, rows, width)
    mine, theirs = pick(wo, core, 0), pick(wo, 1 - core, 0)
    got = swap(theirs, "dp", 1)
    in_keep, in_send = pick(both, low, 0), pick(both, 1 - low, 0)
    out_keep, out_send = jnp.where(low == core, mine, got), jnp.where(low == core, got, mine)
    pairs = []
    per = k_n // 2
    for k in range(0, k_n, per):
        span = slice(k, k + per)
        near = swap(jnp.stack([in_send[span], out_send[span]], 1), "dp", 2)
        for q in range(per):
            mine = jnp.stack([in_keep[k + q], out_keep[k + q]])
            pairs.append((mine, near[q], near))

    where = jnp.stack([me, chip]).astype(jnp.int32)
    halves = [tok[: n_tok // 2], tok[n_tok // 2 :], cot[: n_tok // 2], cot[n_tok // 2 :]]
    far = []

    def spread(k, *others):
        parts = [after(jnp.stack(pairs[k][:2]), *others)]
        flip = 4
        while flip < n_dp:
            parts = parts + [swap(p, "dp", flip) for p in parts]
            flip *= 2
        far.append(parts)

    def near_tokens(i, *others):
        return swap(after(halves[i], *others), "dp", 2)

    spread(0, pairs[0][2])
    t0 = near_tokens(0, where, pairs[0][2])
    t1 = near_tokens(1, far[0][-1], pairs[-1][2])
    spread(1, t0)
    t2 = near_tokens(2, t0)
    t3 = near_tokens(3, t1, far[1][-1])
    spread(2, t2)
    spread(3, t3)
    tok_z, cot_z = [t0, t1], [t2, t3]
    tok_parts = [[tok], [swap(tok, "dp", 1)], tok_z, [swap(p, "dp", 1) for p in tok_z]]
    cot_parts = [[cot], [swap(cot, "dp", 1)], cot_z, [swap(p, "dp", 1) for p in cot_z]]

    merged, seconds = [], []
    holds = {
        3: lambda: [seconds[0]],
    }
    for k in range(k_n):
        down = [1 << b for b in range(members.bit_length() - 1)][::-1]
        up = down[-1:] + down[:-1]
        keep_in, send_in, keep_out, send_out = chunk_call(
            where if k not in holds else after(where, *holds[k]()), tok_parts, cot_parts, far[k], members, chips, scales
        )
        total_in, second = over_members(send_in, keep_in, up)
        total_out, _ = over_members(send_out, keep_out, down)
        seconds.append(second)
        total = jnp.stack([total_in, total_out])
        flip = n_dp // 2
        while flip > 2:
            top = (dp // flip) & 1
            got = swap(half_of(total, 1 - top).astype(BF16), "dp", flip)
            total = half_of(total, top) + got.astype(F32)
            flip //= 2
        merged.append((total[:, :rows] / (total[:, rows:] + 1e-6)).astype(BF16))

    merged = jnp.concatenate(merged, 1)
    got = swap(half_of(merged, 1 - low), "dp", 2)
    merged = half_of(merged, low)
    m_in = jnp.stack([merged[0], got[0]])
    got_in = swap(half_of(m_in, 1 - core), "dp", 1)
    m_in = jnp.stack([half_of(m_in, core), got_in], 1)
    m_in = jnp.where(low == 0, m_in, m_in[::-1])
    m_in = jnp.where(core == 0, m_in, m_in[:, ::-1])
    out_in = m_in.reshape(4 * per_s, d_own).T

    same = low == core
    stay = jnp.where(same, merged[1], got[1])
    got_out = swap(jnp.where(same, got[1], merged[1]), "dp", 1)
    out_out = jnp.where(
        core == 0, jnp.concatenate([stay, got_out]), jnp.concatenate([got_out, stay])
    )
    return out_in, out_out


def solution(mesh):
    spec = P("member", "dp", None)
    return jax.shard_map(
        on_device,
        mesh=mesh,
        in_specs=(spec, spec, spec, spec),
        out_specs=(P("dp", "member"), P("dp", "member")),
        check_vma=False,
    )
```
